32 devices in a mesh: groups: 2 (over y), store: 16 (over z, x, core).
Axes of the slice: x: 2, y: 2, z: 4, core: 2. Of those that a mesh axis runs over, the one named last changes fastest.
Arguments:
- layer_input: bfloat16 [12288, 8192], P('groups', 'store'), parts along dimension 0, may hold values from -6 to 6
- output_grad: bfloat16 [12288, 8192], P('groups', 'store'), parts along dimension 0, may hold values from -6 to 6
- proj_in: bfloat16 [8192, 64], P('store'), may hold values from -0.0625 to 0.0625
- proj_out: bfloat16 [8192, 64], P('store'), may hold values from -0.0625 to 0.0625
- precond_in: float32 [64, 64], replicated
- precond_out: float32 [64, 64], replicated
- query_lengths: int32 [768], P('groups'), parts along dimension 0, may hold values from 1 to 16
- store_rows: bfloat16 [8192, 4096], P('store'), may hold values from -0.0234375 to 0.0234375
- store_live: int32 [16], P('store'), may hold values from 256 to 512, as said below
Outputs:
- scores: float32 [768, 8192], P('groups', 'store'), parts along dimension 0
The draws below stay inside these ranges and needn't reach their ends.
There are 2 independent parts, one for each index of `groups`. The reference program is written for one: setup_inputs(seed, part) draws one part's arguments, and reference() takes and returns one part's arrays. A program takes and returns all parts, laid end to end along the dimension named above; an argument that names none is the same for every part. Nothing has to cross between parts.
Inputs may be any that keep to these rules, and one draw needn't show every extreme that they name: Shard k of the store holds store_live[k] live rows at its head; some shard is full.
All inputs are finite; a program needn't handle non-finite values.
Results may differ from the reference program's by a relative error of at most 0.0029.
Values may be sent and summed in bfloat16 or wider, within the bound.
No kernel may reach another device: no remote copies, remote signals or barrier semaphores. Data moves between devices by JAX's collectives and lax.ppermute only.
A program may use at most 128 MiB of HBM per device.

```python
import math
import jax
import jax.numpy as jnp
from jax import lax

D = 8192
RANK = 64
QLEN = 16
QUERIES = 384
STORE_DEV = 512
GW = 4096
TOKQ = 6144
STORE = 8192
N_STORE = 16


def precond_matrix(key):
    diag_key = jax.random.fold_in(key, 1)
    off_key = jax.random.fold_in(key, 2)
    diagonal = jax.random.uniform(diag_key, (RANK,), jnp.float32, 0.5, 2.0)
    spread = jax.random.normal(off_key, (RANK, RANK), jnp.float32) * (0.4 / math.sqrt(RANK))
    return (jnp.diag(diagonal) + spread).astype(jnp.float32)


def draw_precond_in(key, part):
    return precond_matrix(jax.random.fold_in(key, 11))


def draw_precond_out(key, part):
    return precond_matrix(jax.random.fold_in(key, 23))


def draw_store_live(key, part):
    shards = STORE // STORE_DEV
    counts = jax.random.randint(jax.random.fold_in(key, 5), (shards,), STORE_DEV // 2, STORE_DEV + 1)
    full_shard = jax.random.randint(jax.random.fold_in(key, 7), (), 0, shards)
    return jnp.where(jnp.arange(shards) == full_shard, STORE_DEV, counts).astype(jnp.int32)


def touch_ends(entries, key, smallest, high):
    shape = entries.shape
    spot = [jax.random.randint(jax.random.fold_in(key, axis), (), 0, shape[axis]) for axis in range(len(shape))]
    entries = entries.at[tuple(spot)].set(smallest)
    longest = shape.index(max(shape))
    spot[longest] = (spot[longest] + 1) % shape[longest]
    return entries.at[tuple(spot)].set(high)


def level_of(rng, dims, pieces, smallest, largest):
    gain, own = 1.0, jax.random.fold_in(rng, 6)
    for axis_at, blocks in pieces:
        heights = jnp.exp(jax.random.uniform(jax.random.fold_in(own, axis_at), (blocks,), jnp.float32, smallest / len(pieces), largest / len(pieces)))
        gain = gain * jnp.repeat(heights, dims[axis_at] // blocks).reshape([-1 if axis == axis_at else 1 for axis in range(len(dims))])
    return gain


def gaussian(rng, shape, deviation, reach, cuts=(), kind=jnp.bfloat16):
    entries = jax.random.normal(rng, shape, jnp.float32) * deviation
    if len(cuts) > 0:
        entries = level_of(rng, shape, cuts, -0.22, 0.18) * entries
    return jnp.clip(entries, min=-reach, max=reach).astype(kind)


def setup_inputs(seed: int = 0, part: int = 0) -> dict:
    seeds = jax.random.split(jax.random.key(seed), 10)
    part_splits = jax.random.split(jax.random.fold_in(seeds[9], part), 10)
    return {
        "layer_input": gaussian(part_splits[0], (TOKQ, D), 1.0, 6.0, ((1, 16),)),
        "output_grad": gaussian(part_splits[1], (TOKQ, D), 1.0, 6.0, ((1, 16),)),
        "proj_in": gaussian(seeds[2], (D, RANK), D ** -0.5, 0.0625, ((0, 16),)),
        "proj_out": gaussian(seeds[3], (D, RANK), D ** -0.5, 0.0625, ((0, 16),)),
        "precond_in": draw_precond_in(jax.random.fold_in(seeds[9], 71), part),
        "precond_out": draw_precond_out(jax.random.fold_in(seeds[9], 71), part),
        "query_lengths": touch_ends(jax.random.randint(part_splits[6], (QUERIES,), 1, QLEN + 1), jax.random.fold_in(part_splits[6], 1), 1, QLEN).astype(jnp.int32),
        "store_rows": gaussian(seeds[7], (STORE, GW), (1.0 / (4 * RANK)), 0.0234375, ((0, 16),)),
        "store_live": draw_store_live(jax.random.fold_in(seeds[9], 71), part),
    }


def precondition(factors, lengths, precond_in, precond_out):
    query_count = lengths.shape[0]
    proj_rank = precond_in.shape[0]
    query_len = factors.shape[0] // query_count
    token_keep = (jnp.arange(query_len, dtype=jnp.int32)[None, :] < lengths[:, None]).astype(jnp.float32)
    input_side = factors[:, :proj_rank].reshape(query_count, query_len, proj_rank) * token_keep[:, :, None]
    output_side = factors[:, proj_rank:].reshape(query_count, query_len, proj_rank)
    outer_sums = jnp.einsum("qti,qtj->qij", input_side, output_side, precision=lax.Precision.HIGHEST)
    left_side = jnp.einsum("ai,qij->qaj", precond_in, outer_sums, precision=lax.Precision.HIGHEST)
    conditioned = jnp.einsum("qaj,jb->qab", left_side, precond_out, precision=lax.Precision.HIGHEST)
    return conditioned.reshape(query_count, proj_rank * proj_rank).astype(jnp.bfloat16)


def reference(layer_input, output_grad, proj_in, proj_out, precond_in, precond_out, query_lengths, store_rows, store_live):
    input_low = jnp.dot(layer_input, proj_in, preferred_element_type=jnp.float32)
    output_low = jnp.dot(output_grad, proj_out, preferred_element_type=jnp.float32)
    factors = jnp.concatenate([input_low, output_low], axis=1)
    query_grads = precondition(factors, query_lengths, precond_in, precond_out).astype(jnp.float32)
    blocks = store_rows.reshape(N_STORE, STORE_DEV, GW)
    row_index = jnp.arange(STORE_DEV, dtype=jnp.int32)

    def one_block(packed):
        block_rows, live_rows = packed
        products = lax.dot_general(query_grads, block_rows.astype(jnp.float32), (((1,), (1,)), ((), ())), precision=lax.Precision.HIGHEST)
        return jnp.where(row_index[None, :] < live_rows, products, 0.0)

    result = lax.map(one_block, (blocks, store_live))
    return jnp.transpose(result, (1, 0, 2)).reshape(QUERIES, N_STORE * STORE_DEV)
```

```python
import functools

import jax
import jax.numpy as jnp
import numpy as np
from jax import lax
from jax.experimental import pallas as pl
from jax.experimental.pallas import tpu as pltpu
from jax.sharding import PartitionSpec as P


SPAN = 32768.0
SCALE_ROWS = 16


def chip_ring(mesh):
    chips = mesh.shape["store"] // 2
    first_group = mesh.devices.reshape(mesh.shape["groups"], mesh.shape["store"])[0]
    coords = [getattr(d, "coords", None) for d in first_group[::2]]
    width = len({c[0] for c in coords}) if coords[0] is not None else 2
    depth = chips // width
    if width * depth != chips or width < 2 or depth % 2:
        return list(range(chips))
    order = [z * width for z in range(depth)]
    for step, z in enumerate(reversed(range(depth))):
        xs = range(1, width)
        order += [z * width + x for x in (xs if step % 2 == 0 else reversed(xs))]
    return order


def project_kernel(first_ref, x_ref, g_ref, win_ref, wout_ref, out_ref, w_scr):
    @pl.when(pl.program_id(0) == 0)
    def _():
        rank = win_ref.shape[0]
        w_scr[...] = jnp.zeros_like(w_scr)
        w_scr[0, :rank, :] = win_ref[...]
        w_scr[1, rank:, :] = wout_ref[...]

    dims = (((1,), (1,)), ((), ()))
    out_ref[...] = lax.dot_general(
        x_ref[...], w_scr[0], dims, preferred_element_type=jnp.float32
    ) + lax.dot_general(g_ref[...], w_scr[1], dims, preferred_element_type=jnp.float32)


def project_half(first_block, blocks, tm, x, g, win_t, wout_t):
    feat = x.shape[1]
    rank = win_t.shape[0]
    rows = blocks * tm
    return pl.pallas_call(
        project_kernel,
        out_shape=jax.ShapeDtypeStruct((rows, 2 * rank), jnp.float32),
        grid_spec=pltpu.PrefetchScalarGridSpec(
            num_scalar_prefetch=1,
            grid=(blocks,),
            in_specs=[
                pl.BlockSpec((tm, feat), lambda i, f: (f[0] + i, 0)),
                pl.BlockSpec((tm, feat), lambda i, f: (f[0] + i, 0)),
                pl.BlockSpec((rank, feat), lambda i, f: (0, 0)),
                pl.BlockSpec((rank, feat), lambda i, f: (0, 0)),
            ],
            out_specs=pl.BlockSpec((tm, 2 * rank), lambda i, f: (i, 0)),
            scratch_shapes=[pltpu.VMEM((2, 2 * rank, feat), jnp.bfloat16)],
        ),
        cost_estimate=pl.CostEstimate(
            flops=4 * rows * feat * rank, bytes_accessed=4 * rows * feat, transcendentals=0
        ),
    )(first_block, x, g, win_t, wout_t)


def combine_kernel(chunk_ref, mine_ref, theirs_ref, out_ref):
    total = mine_ref[...] + theirs_ref[...]
    rows = total.shape[0]
    largest = jnp.max(jnp.abs(total), axis=0, keepdims=True)
    largest = jnp.maximum(largest, 1e-30)
    out_ref[0, :rows, :] = total
    out_ref[0, rows:, :] = jnp.broadcast_to(
        jnp.ceil(jnp.log2(largest)) + 1.0, (SCALE_ROWS, total.shape[1])
    )


def combine(order, mine, theirs, slots):
    rows = mine.shape[0] // slots
    width = mine.shape[1]
    spec = pl.BlockSpec((rows, width), lambda i, c: (c[i], 0))
    return pl.pallas_call(
        combine_kernel,
        out_shape=jax.ShapeDtypeStruct((slots, rows + SCALE_ROWS, width), jnp.float32),
        grid_spec=pltpu.PrefetchScalarGridSpec(
            num_scalar_prefetch=1,
            grid=(slots,),
            in_specs=[spec, spec],
            out_specs=pl.BlockSpec((1, rows + SCALE_ROWS, width), lambda i, c: (i, 0, 0)),
        ),
    )(order, mine, theirs)


def encode(padded):
    rows = padded.shape[0] - SCALE_ROWS
    exponent = padded[rows : rows + 1]
    is_row = lax.broadcasted_iota(jnp.int32, padded.shape, 0) < rows
    return jnp.where(is_row, padded * (jnp.exp2(-exponent) * SPAN), padded).astype(jnp.float16)


def decode(payload):
    rows = payload.shape[0] - SCALE_ROWS
    wide = payload.astype(jnp.float32)
    exponent = wide[rows : rows + 1]
    is_row = lax.broadcasted_iota(jnp.int32, payload.shape, 0) < rows
    return jnp.where(is_row, wide * (jnp.exp2(exponent) * (1.0 / SPAN)), wide)


def add_padded(a, b):
    rows = a.shape[0] - SCALE_ROWS
    is_row = lax.broadcasted_iota(jnp.int32, a.shape, 0) < rows
    return jnp.where(is_row, a + b, jnp.maximum(a, b) + 1.0)


def grads_kernel(sums_ref, keep_ref, mix_ref, out_ref, fac_scr, grad_scr):
    rank = mix_ref.shape[0] // 2
    queries = out_ref.shape[0]
    slots = sums_ref.shape[0] // queries
    fac_scr[...] = (
        jnp.dot(
            sums_ref[...],
            mix_ref[...],
            precision=lax.Precision.HIGHEST,
            preferred_element_type=jnp.float32,
        )
        * keep_ref[...]
    )
    left = lax.broadcasted_iota(jnp.int32, (8, 2 * rank), 1) < rank
    pairs = 8

    def group(g, carry):
        facs = [fac_scr[pl.ds(g * 8 * slots + t, 8, stride=slots), :] for t in range(slots)]
        outs = [jnp.where(left, pltpu.roll(f, rank, 1), f) for f in facs]
        for block in range(0, rank // 2, pairs):
            acc = [None] * pairs
            for t in range(slots):
                for p in range(pairs):
                    i = 2 * (block + p)
                    a0 = jnp.broadcast_to(facs[t][:, i : i + 1], (8, 2 * rank))
                    a1 = jnp.broadcast_to(facs[t][:, i + 1 : i + 2], (8, 2 * rank))
                    term = jnp.where(left, a0, a1) * outs[t]
                    acc[p] = term if acc[p] is None else acc[p] + term
            for p in range(pairs):
                i = 2 * (block + p)
                grad_scr[pl.ds(g * 8, 8), i * rank : (i + 2) * rank] = acc[p]
        return carry

    lax.fori_loop(0, queries // 8, group, 0)
    out_ref[...] = grad_scr[...].astype(out_ref.dtype)


def query_grads_of(sums, keep, mix, queries):
    rank = mix.shape[0] // 2
    if queries % 8 == 0:
        return pl.pallas_call(
            grads_kernel,
            out_shape=jax.ShapeDtypeStruct((queries, rank * rank), jnp.bfloat16),
            scratch_shapes=[
                pltpu.VMEM(sums.shape, jnp.float32),
                pltpu.VMEM((queries, rank * rank), jnp.float32),
            ],
        )(sums, keep, mix)
    fac = jnp.dot(sums, mix, precision=lax.Precision.HIGHEST) * keep
    fac = fac.reshape(queries, -1, 2 * rank)
    grads = jnp.einsum(
        "qti,qtj->qij", fac[:, :, :rank], fac[:, :, rank:], precision=lax.Precision.HIGHEST
    )
    return grads.reshape(queries, rank * rank).astype(jnp.bfloat16)


def score_kernel(first_ref, live_ref, grads_ref, rows_ref, out_ref):
    chunk = grads_ref.shape[1]
    grads = grads_ref[...].reshape(-1, grads_ref.shape[2])
    products = lax.dot_general(
        grads, rows_ref[...], (((1,), (1,)), ((), ())), preferred_element_type=jnp.float32
    )
    column = lax.broadcasted_iota(jnp.int32, products.shape, 1)
    products = jnp.where(column < live_ref[0], products, 0.0)
    for c in range(grads_ref.shape[0]):
        start = pl.multiple_of(first_ref[c], 8)
        out_ref[pl.ds(start, chunk), :] = products[c * chunk : (c + 1) * chunk]


def score(first_rows, live, grads, store_rows):
    total = grads.shape[0] * grads.shape[1]
    if grads.shape[1] % 8 == 0:
        smem = pl.BlockSpec(memory_space=pltpu.SMEM)
        vmem = pl.BlockSpec(memory_space=pltpu.VMEM)
        return pl.pallas_call(
            score_kernel,
            out_shape=jax.ShapeDtypeStruct((total, store_rows.shape[0]), jnp.float32),
            in_specs=[smem, smem, vmem, vmem],
            out_specs=vmem,
        )(first_rows, live, grads, store_rows)
    chunk = grads.shape[1]
    place = (first_rows[:, None] + jnp.arange(chunk)[None, :]).reshape(-1)
    products = lax.dot_general(
        grads.reshape(total, -1),
        store_rows,
        (((1,), (1,)), ((), ())),
        preferred_element_type=jnp.float32,
    )
    column = jnp.arange(store_rows.shape[0], dtype=jnp.int32)
    products = jnp.where(column[None, :] < live[0], products, 0.0)
    return jnp.zeros_like(products).at[place].set(products)


def local(
    ring,
    layer_input,
    output_grad,
    proj_in,
    proj_out,
    precond_in,
    precond_out,
    query_lengths,
    store_rows,
    store_live,
):
    chips = len(ring)
    devices = 2 * chips
    tokens = layer_input.shape[0]
    queries = query_lengths.shape[0]
    slots = tokens // queries
    rank = proj_in.shape[1]
    my_queries = queries // devices
    chunk = tokens // devices

    index = lax.axis_index("store")
    core = index % 2
    places = np.argsort(np.asarray(ring))
    place = jnp.int32(0)
    for chip in range(chips):
        place = jnp.where(index // 2 == chip, jnp.int32(places[chip]), place)

    other_core = [(d, d ^ 1) for d in range(devices)]

    def along(step):
        return [
            (ring[p] * 2 + k, ring[(p + step) % chips] * 2 + k)
            for p in range(chips)
            for k in range(2)
        ]

    send = functools.partial(lax.ppermute, axis_name="store")

    tm = tokens // 16
    blocks = 8
    win_t, wout_t = proj_in.T, proj_out.T
    for_other = project_half(
        jnp.reshape((1 - core) * blocks, (1,)), blocks, tm, layer_input, output_grad, win_t, wout_t
    )
    from_other = send(for_other, perm=other_core)
    mine = project_half(
        jnp.reshape(core * blocks, (1,)), blocks, tm, layer_input, output_grad, win_t, wout_t
    )

    up = chips // 2
    down = chips - 1 - up
    offsets = [0] + [d for s in range(up) for d in (up - s, -(down - s)) if d > 0 or s < down]
    order = jnp.stack([(place + d + chips) % chips for d in offsets]).astype(jnp.int32)
    held = combine(order, mine, from_other, chips)
    slot_of = {d: held[i] for i, d in enumerate(offsets)}

    up_value = down_value = None
    for s in range(up):
        part = slot_of[up - s]
        if up_value is not None:
            part = add_padded(part, decode(up_value))
        up_value = send(encode(part), perm=along(1))
        if s < down:
            part = slot_of[-(down - s)]
            if down_value is not None:
                part = add_padded(part, decode(down_value))
            down_value = send(encode(part), perm=along(-1))
    sums = (slot_of[0] + decode(up_value) + decode(down_value))[:chunk]

    first_query = (core * chips + place) * my_queries
    my_lengths = lax.dynamic_slice_in_dim(query_lengths, first_query, my_queries, 0)
    keep = (jnp.arange(slots, dtype=jnp.int32)[None, :] < my_lengths[:, None]).astype(jnp.float32)
    keep = jnp.broadcast_to(keep[:, :, None], (my_queries, slots, 2 * rank)).reshape(chunk, 2 * rank)
    zero = jnp.zeros((rank, rank), jnp.float32)
    mix = jnp.block([[precond_in.T, zero], [zero, precond_out]])
    grads = query_grads_of(sums, keep, mix, my_queries)

    gathered = [grads]
    order_of = [place]
    up_value = down_value = grads
    for s in range(up):
        up_value = send(up_value, perm=along(1))
        gathered.append(up_value)
        order_of.append((place - s - 1 + chips) % chips)
        if s < down:
            down_value = send(down_value, perm=along(-1))
            gathered.append(down_value)
            order_of.append((place + s + 1) % chips)
    half = jnp.stack(gathered)
    other_half = send(half, perm=other_core)
    order_of = jnp.stack(order_of)
    starts = jnp.concatenate(
        [(core * chips + order_of) * my_queries, ((1 - core) * chips + order_of) * my_queries]
    ).astype(jnp.int32)
    return score(starts, store_live, jnp.concatenate([half, other_half]), store_rows)


def solution(mesh):
    placed = (
        P("groups", "store"),
        P("groups", "store"),
        P("store", None),
        P("store", None),
        P(),
        P(),
        P("groups"),
        P("store", None),
        P("store"),
    )
    return jax.shard_map(
        functools.partial(local, chip_ring(mesh)),
        mesh=mesh,
        in_specs=placed,
        out_specs=P("groups", "store"),
        check_vma=False,
    )
```
